32 devices in a mesh: grp: 4 (over z), inner: 8 (over y, x, core).
Axes of the slice: x: 2, y: 2, z: 4, core: 2. Of those that a mesh axis runs over, the one named last changes fastest.
Arguments:
- design: float32 [8, 4096, 1024], P('inner', 'grp'), may hold values from -6 to 6
- row_signs: int32 [8, 4096], P('inner', 'grp'), may hold values from 0 to 1
- kept_rows: int32 [8, 2048], P('inner'), may hold values from 0 to 4095, as said below
Outputs:
- factored: float32 [2048, 1024], P('grp')
The draws below stay inside these ranges and needn't reach their ends.
Inputs may be any that keep to these rules, and one draw needn't show every extreme that they name: `kept_rows`: within each block the 2048 kept row numbers are distinct, and each block keeps its first and its last row.
All inputs are finite; a program needn't handle non-finite values.
Results may differ from the reference program's by a relative error of at most 0.0048.
Values may be sent and summed in bfloat16 or wider, within the bound.
No kernel may reach another device: no remote copies, remote signals or barrier semaphores. Data moves between devices by JAX's collectives and lax.ppermute only.
A program may use at most 64 MiB of HBM per device.

```python
import math
import jax
import jax.numpy as jnp
from jax import lax

D = 1024
BLOCK = 4096
KEEP = 2048
COLS_DONE = 8
NBLOCKS = 8


def draw_kept_rows(key, part):

    def draw_block(block_key):
        order_key, shuffle_key = jax.random.split(block_key)
        inner_rows = jax.random.permutation(order_key, BLOCK - 2)[:KEEP - 2].astype(jnp.int32) + 1
        kept_list = jnp.concatenate([inner_rows, jnp.array([0, BLOCK - 1], dtype=jnp.int32)])
        return jax.random.permutation(shuffle_key, kept_list)
    block_keys = jax.random.split(jax.random.fold_in(key, 17), NBLOCKS)
    return jax.vmap(draw_block)(block_keys).astype(jnp.int32)


def place_ends(entries, own_key, low, largest):
    place = [jax.random.randint(jax.random.fold_in(own_key, axis), (), 0, length) for axis, length in enumerate(entries.shape)]
    main_axis = entries.shape.index(max(entries.shape))
    neighbour = place[:main_axis] + [(place[main_axis] + 1) % entries.shape[main_axis]] + place[main_axis + 1:]
    return entries.at[tuple(place)].set(low).at[tuple(neighbour)].set(largest)


def steps_of(rng, extent, cuts, least, high):
    gain = 1.0
    for position, parts in cuts:
        draws = jax.random.uniform(jax.random.fold_in(jax.random.fold_in(rng, 6), position), (parts,), jnp.float32, least / len(cuts), high / len(cuts))
        gain = gain * jnp.repeat(jnp.exp(draws), extent[position] // parts).reshape((-1,) + (1,) * (len(extent) - 1 - position))
    return gain


def scatter_about(own_key, extent, spread, reach, shards=(), kind=jnp.bfloat16):
    loudness = steps_of(own_key, extent, shards, -0.22, 0.18) if shards else 1.0
    values = jax.random.normal(own_key, extent, jnp.float32) * spread * loudness
    return jnp.minimum(jnp.maximum(values, -reach), reach).astype(kind)


def setup_inputs(seed: int = 0) -> dict:
    keys = jax.random.split(jax.random.key(seed), 4)
    design = scatter_about(keys[0], (NBLOCKS, BLOCK, D), 1.0, 6.0, ((0, 8), (1, 4)), jnp.float32)
    row_signs = place_ends(jax.random.randint(keys[1], (NBLOCKS, BLOCK), 0, 2), jax.random.fold_in(keys[1], 1), 0, 1).astype(jnp.int32)
    kept_rows = draw_kept_rows(jax.random.fold_in(keys[3], 71), 0)
    return {"design": design, "row_signs": row_signs, "kept_rows": kept_rows}


epsilon = 1e-06

def sign_table(row_ids, col_ids):
    common_bits = jnp.bitwise_and(row_ids[:, None], col_ids[None, :])
    ones_total = jnp.zeros(common_bits.shape, jnp.int32)
    for bit_pos in range(4):
        ones_total = ones_total + jnp.bitwise_and(jnp.right_shift(common_bits, bit_pos), 1)
    return 1.0 - 2.0 * jnp.bitwise_and(ones_total, 1).astype(jnp.float32)

def reference(design, row_signs, kept_rows):
    columns = design.shape[2]
    sixteen = jnp.arange(16, dtype=jnp.int32)
    hadamard = sign_table(sixteen, sixteen)
    highest = lax.Precision.HIGHEST

    def one_block(total, items):
        block_rows, flips, chosen = items
        flipped = (block_rows * (1 - 2 * flips).astype(jnp.float32)[:, None]).astype(jnp.bfloat16)
        lowest = lax.optimization_barrier(flipped).astype(jnp.float32).reshape(BLOCK // 16, 16, columns)
        first_pass = jnp.einsum('hc,ncd->nhd', hadamard, lowest, precision=highest).astype(jnp.bfloat16)
        middle_view = lax.optimization_barrier(first_pass).astype(jnp.float32).reshape(16, 16, 16, columns)
        second_pass = jnp.einsum('hb,abcd->ahcd', hadamard, middle_view, precision=highest).astype(jnp.bfloat16)
        top_view = lax.optimization_barrier(second_pass).astype(jnp.float32).reshape(16, 16, 16, columns)
        mixed_rows = jnp.einsum('ha,abcd->hbcd', hadamard, top_view, precision=highest).reshape(BLOCK, columns)
        return (total + jnp.take(mixed_rows, chosen.astype(jnp.int32), axis=0), None)
    start_total = jnp.zeros((KEEP, columns), jnp.float32)
    total, unused = lax.scan(one_block, start_total, (design, row_signs, kept_rows))
    sketch = total * (1.0 / (64.0 * math.sqrt(KEEP)))
    row_ids = jnp.arange(KEEP, dtype=jnp.int32)

    def reflect(col_index, current):
        column = jnp.where(row_ids >= col_index, current[:, col_index], 0.0)
        norm_sq = jnp.sum(column * column)
        pivot_value = current[col_index, col_index]
        head_value = -jnp.where(pivot_value >= 0, 1.0, -1.0) * jnp.sqrt(norm_sq)
        vector = column - head_value * (row_ids == col_index).astype(jnp.float32)
        length = 2.0 * (norm_sq - head_value * pivot_value) + epsilon
        projected_row = jnp.dot(vector, current, precision=highest)
        return current - vector[:, None] * (2.0 * projected_row / length)[None, :]
    return lax.fori_loop(0, COLS_DONE, reflect, sketch)
```

```python
import functools
import math

import jax
import jax.numpy as jnp
from jax import lax
from jax.experimental import pallas as pl
from jax.experimental.pallas import tpu as pltpu
from jax.sharding import PartitionSpec as P

COLS_DONE = 8
LANES = 128
LOW = 256

epsilon = 1e-06


def sign_table(row_ids, col_ids):
    common_bits = jnp.bitwise_and(row_ids[:, None], col_ids[None, :])
    ones_total = jnp.zeros(common_bits.shape, jnp.int32)
    for bit_pos in range(4):
        ones_total = ones_total + jnp.bitwise_and(jnp.right_shift(common_bits, bit_pos), 1)
    return 1.0 - 2.0 * jnp.bitwise_and(ones_total, 1).astype(jnp.float32)


def pick_rows(table_rows, chosen_rows):
    return jnp.take(table_rows, chosen_rows, axis=0)


def plain_form(design, row_signs, kept_rows):
    block_count, local_rows, columns = design.shape
    keep_count = kept_rows.shape[1]
    groups = lax.axis_size("grp")
    owned_rows = keep_count // groups
    highest = lax.Precision.HIGHEST
    sixteen = jnp.arange(16, dtype=jnp.int32)
    hadamard = sign_table(sixteen, sixteen).astype(jnp.bfloat16)
    flipped = (design * (1 - 2 * row_signs).astype(jnp.float32)[:, :, None]).astype(jnp.bfloat16)
    lowest = flipped.reshape(block_count * local_rows // 16, 16, columns)
    first_pass = jnp.einsum(
        "hc,ncd->nhd", hadamard, lowest, preferred_element_type=jnp.float32
    ).astype(jnp.bfloat16)
    middle_view = first_pass.reshape(block_count * local_rows // 256, 16, 16, columns)
    second_pass = jnp.einsum(
        "hb,mbcd->mhcd", hadamard, middle_view, preferred_element_type=jnp.float32
    ).astype(jnp.bfloat16)
    second_pass = second_pass.reshape(block_count, local_rows, columns)
    gathered_rows = lax.all_to_all(second_pass, "grp", split_axis=2, concat_axis=1, tiled=True)
    col_count = gathered_rows.shape[2]
    by_piece = gathered_rows.reshape(block_count, 16, 256, col_count)
    mixed_rows = jnp.einsum("ha,nakd->nhkd", hadamard, by_piece, preferred_element_type=jnp.float32)
    mixed_rows = mixed_rows.reshape(block_count, 16 * 256, col_count)
    picked = jax.vmap(pick_rows)(mixed_rows, kept_rows)
    partial_value = jnp.sum(picked, axis=0)
    summed = lax.psum(partial_value, "inner")
    sketch = lax.all_to_all(summed, "grp", split_axis=0, concat_axis=1, tiled=True)
    sketch = sketch * (1.0 / (64.0 * math.sqrt(keep_count)))
    row_base = lax.axis_index("grp") * owned_rows
    global_rows = row_base + jnp.arange(owned_rows, dtype=jnp.int32)

    def reflect(col_index, current):
        column = jnp.where(global_rows >= col_index, current[:, col_index], 0.0)
        is_pivot = (global_rows == col_index).astype(jnp.float32)
        norm_sq, crossed, pivot_row = lax.psum(
            (
                jnp.sum(column * column),
                jnp.dot(column, current, precision=highest),
                jnp.dot(is_pivot, current, precision=highest),
            ),
            "grp",
        )
        pivot_value = pivot_row[col_index]
        head_value = -jnp.where(pivot_value >= 0, 1.0, -1.0) * jnp.sqrt(norm_sq)
        length = 2.0 * (norm_sq - head_value * pivot_value) + epsilon
        projected_row = crossed - head_value * pivot_row
        vector = column - head_value * is_pivot
        return current - vector[:, None] * (2.0 * projected_row / length)[None, :]

    return lax.fori_loop(0, COLS_DONE, reflect, sketch)


def swap(value, axis, mask):
    pairs = [(place, place ^ mask) for place in range(lax.axis_size(axis))]
    return lax.ppermute(value, axis, pairs)


def odd_ones(bits):
    bits = bits ^ (bits >> 2)
    bits = bits ^ (bits >> 1)
    return bits & 1


def low_hadamard(shift):
    row = lax.broadcasted_iota(jnp.int32, (LOW, LOW), 0)
    col = lax.broadcasted_iota(jnp.int32, (LOW, LOW), 1)
    signs = 1 - 2 * odd_ones((row & col) >> shift & 15)
    same = ((row ^ col) & (255 - (15 << shift))) == 0
    return jnp.where(same, signs, 0).astype(jnp.float32)


def passes(signs_ref, data_refs, mixed_ref):
    inner_table = low_hadamard(0)
    outer_table = low_hadamard(4).astype(jnp.bfloat16)
    for piece in range(mixed_ref.shape[0] // LOW):
        rows = pl.ds(piece * LOW, LOW)
        flips = (1 - 2 * signs_ref[:, rows]).astype(jnp.float32)
        table = (inner_table * flips).astype(jnp.bfloat16)
        data = jnp.concatenate([ref[rows, :].astype(jnp.bfloat16) for ref in data_refs], axis=1)
        first = jnp.dot(table, data, preferred_element_type=jnp.float32).astype(jnp.bfloat16)
        second = jnp.dot(outer_table, first, preferred_element_type=jnp.float32)
        mixed_ref[rows, :] = second.astype(jnp.bfloat16)


def choice(kept_ref, first_piece, pieces):
    kept = jnp.broadcast_to(kept_ref[...], (8, kept_ref.shape[1]))
    line = lax.broadcasted_iota(jnp.int32, kept.shape, 0)
    signs = 1 - 2 * odd_ones((kept >> 8) & (first_piece + line))
    packed = jnp.where(line < pieces, signs, kept & 255).astype(jnp.float32)
    tall = packed.T
    lane = lax.broadcasted_iota(jnp.int32, (kept.shape[1], LOW), 1).astype(jnp.float32)
    hit = tall[:, pieces : pieces + 1] == lane
    parts = [jnp.where(hit, tall[:, piece : piece + 1], 0.0).astype(jnp.bfloat16) for piece in range(pieces)]
    return jnp.concatenate(parts, axis=1)


def contribution_kernel(pieces, place_ref, kept_ref, signs_ref, *refs):
    *data_refs, out_ref, mixed_ref = refs

    @pl.when(pl.program_id(0) == 0)
    def _():
        passes(signs_ref, data_refs, mixed_ref)

    table = choice(kept_ref, place_ref[1] * pieces, pieces)
    part = jnp.dot(table, mixed_ref[...], preferred_element_type=jnp.float32)
    width = data_refs[0].shape[1]
    for index in range(len(data_refs)):
        out_ref[index] = part[:, index * width : (index + 1) * width].astype(out_ref.dtype)


def contribution(place, kept, signs, data, width, masks, dtype, steps=4):
    rows, keep = data.shape[0], kept.shape[1]
    tall = keep // steps

    def column_group(mask):
        return pl.BlockSpec((rows, width), lambda s, place_ref: (0, place_ref[0] ^ mask))

    return pl.pallas_call(
        functools.partial(contribution_kernel, rows // LOW),
        out_shape=jax.ShapeDtypeStruct((len(masks), keep, width), dtype),
        grid_spec=pltpu.PrefetchScalarGridSpec(
            num_scalar_prefetch=1,
            grid=(steps,),
            in_specs=[
                pl.BlockSpec((1, tall), lambda s, place_ref: (0, s)),
                pl.BlockSpec((1, rows), lambda s, place_ref: (0, 0)),
            ]
            + [column_group(mask) for mask in masks],
            out_specs=pl.BlockSpec((len(masks), tall, width), lambda s, place_ref: (0, s, 0)),
            scratch_shapes=[pltpu.VMEM((rows, len(masks) * width), jnp.bfloat16)],
        ),
        name="contribution",
    )(place, kept, signs, *([data] * len(masks)))


def panel_kernel(pieces, place_ref, kept_ref, signs_ref, data_ref, out_ref, mixed_ref):
    @pl.when(pl.program_id(0) == 0)
    def _():
        passes(signs_ref, [data_ref], mixed_ref)

    table = choice(kept_ref, place_ref[1] * pieces, pieces)
    part = jnp.dot(table, mixed_ref[...], preferred_element_type=jnp.float32)
    out_ref[...] = part.T[:COLS_DONE, :]


def panel_contribution(place, kept, signs, data, steps=4):
    rows, keep = data.shape[0], kept.shape[1]
    tall = keep // steps
    return pl.pallas_call(
        functools.partial(panel_kernel, rows // LOW),
        out_shape=jax.ShapeDtypeStruct((COLS_DONE, keep), jnp.float32),
        grid_spec=pltpu.PrefetchScalarGridSpec(
            num_scalar_prefetch=1,
            grid=(steps,),
            in_specs=[
                pl.BlockSpec((1, tall), lambda s, place_ref: (0, s)),
                pl.BlockSpec((1, rows), lambda s, place_ref: (0, 0)),
                pl.BlockSpec((rows, LANES), lambda s, place_ref: (0, 0)),
            ],
            out_specs=pl.BlockSpec((COLS_DONE, tall), lambda s, place_ref: (0, s)),
            scratch_shapes=[pltpu.VMEM((rows, LANES), jnp.bfloat16)],
        ),
        name="panel",
    )(place, kept, signs, data)


def factor_kernel(scale, panel_ref, vectors_ref, weights_ref):
    current = panel_ref[...] * scale
    count, keep = current.shape
    lane = lax.broadcasted_iota(jnp.int32, (1, keep), 1)
    line = lax.broadcasted_iota(jnp.int32, (count, 1), 0)
    short = lax.broadcasted_iota(jnp.int32, (1, LANES), 1)
    vectors = jnp.zeros((count, keep), jnp.float32)
    weights = jnp.zeros((count, LANES), jnp.float32)
    for j in range(count):
        column = jnp.where(lane >= j, current[j : j + 1, :], 0.0)
        is_pivot = lane == j
        crossed = jnp.sum(current * column, axis=1, keepdims=True)
        pivot_row = jnp.sum(jnp.where(is_pivot, current, 0.0), axis=1, keepdims=True)
        norm_sq = crossed[j : j + 1, :]
        pivot = pivot_row[j : j + 1, :]
        head = jnp.where(pivot >= 0, -1.0, 1.0) * jnp.sqrt(norm_sq)
        length = 2.0 * (norm_sq - head * pivot) + epsilon
        vector = column - jnp.where(is_pivot, head, 0.0)
        projected = crossed - head * pivot_row
        current = current - (2.0 * projected / length) * vector
        shared = jnp.sum(vectors * vector, axis=1, keepdims=True)
        unit = jnp.where(short == j, 1.0, 0.0)
        row = (2.0 / length) * (unit - jnp.sum(shared * weights, axis=0, keepdims=True))
        vectors = jnp.where(line == j, vector, vectors)
        weights = jnp.where(line == j, row, weights)
    vectors_ref[...] = vectors
    weights_ref[...] = weights


def factor(panel, scale):
    count, keep = panel.shape
    return pl.pallas_call(
        functools.partial(factor_kernel, scale),
        out_shape=(
            jax.ShapeDtypeStruct((count, keep), jnp.float32),
            jax.ShapeDtypeStruct((count, LANES), jnp.float32),
        ),
        name="factor",
    )(panel)


def split_two(value):
    high = value.astype(jnp.bfloat16)
    low = (value - high.astype(jnp.float32)).astype(jnp.bfloat16)
    return jnp.concatenate([high, low], axis=0)


def spread_kernel(scale, arrived_count, place_ref, vectors_ref, base_ref, *refs):
    arrived, outs = refs[:arrived_count], refs[arrived_count:]
    *send_refs, own_ref, product_ref = outs
    rows = own_ref.shape[0]
    count = vectors_ref.shape[0]

    def total(window):
        value = base_ref[window, :]
        for ref in arrived:
            value = value + ref[window, :].astype(jnp.float32)
        return value * scale

    whole = total(slice(None)).astype(jnp.bfloat16)
    both = jnp.dot(split_two(vectors_ref[...]), whole, preferred_element_type=jnp.float32)
    product = both[:count] + both[count:]
    product_ref[...] = product
    pair = split_two(product)

    def window_of(mask):
        return pl.ds(pl.multiple_of((place_ref[1] ^ mask) * rows, rows), rows)

    own_ref[...] = total(window_of(0))
    for index, send_ref in enumerate(send_refs):
        send_ref[:rows, :] = total(window_of(index + 1)).astype(jnp.bfloat16)
        send_ref[rows:, :] = pair


def spread(place, vectors, base, arrived, groups, scale):
    keep, width = base.shape
    count = vectors.shape[0]
    rows = keep // groups
    vmem = pl.BlockSpec(memory_space=pltpu.VMEM)
    outs = [jax.ShapeDtypeStruct((rows + 2 * count, width), jnp.bfloat16)] * (groups - 1)
    outs += [jax.ShapeDtypeStruct((rows, width), jnp.float32), jax.ShapeDtypeStruct((count, width), jnp.float32)]
    return pl.pallas_call(
        functools.partial(spread_kernel, scale, len(arrived)),
        out_shape=tuple(outs),
        in_specs=[pl.BlockSpec(memory_space=pltpu.SMEM)] + [vmem] * (2 + len(arrived)),
        out_specs=(vmem,) * len(outs),
        name="spread",
    )(place, vectors, base, *arrived)


def apply_kernel(place_ref, vectors_ref, weights_ref, own_ref, product_ref, *refs):
    *arrived, out_ref = refs
    rows = own_ref.shape[0]
    count = vectors_ref.shape[0]
    value = own_ref[...]
    product = product_ref[...]
    for ref in arrived:
        value = value + ref[:rows, :].astype(jnp.float32)
        pair = ref[rows:, :].astype(jnp.float32)
        product = product + (pair[:count] + pair[count:])
    highest = lax.Precision.HIGHEST
    multipliers = jnp.dot(
        weights_ref[:, :count], product, precision=highest, preferred_element_type=jnp.float32
    )
    window = pl.ds(pl.multiple_of(place_ref[1] * rows, rows), rows)
    vectors = vectors_ref[:, window]
    update = lax.dot_general(
        vectors, multipliers, (((0,), (0,)), ((), ())), precision=highest, preferred_element_type=jnp.float32
    )
    out_ref[...] = (value - update).astype(jnp.bfloat16)


def apply(place, vectors, weights, own, product, arrived):
    vmem = pl.BlockSpec(memory_space=pltpu.VMEM)
    return pl.pallas_call(
        apply_kernel,
        out_shape=jax.ShapeDtypeStruct(own.shape, jnp.bfloat16),
        in_specs=[pl.BlockSpec(memory_space=pltpu.SMEM)] + [vmem] * (4 + len(arrived)),
        out_specs=vmem,
        name="apply",
    )(place, vectors, weights, own, product, *arrived)


def lay_kernel(masks, place_ref, *refs):
    *parts, out_ref = refs
    width = parts[0].shape[1]
    for mask, ref in zip(masks, parts):
        start = pl.multiple_of((place_ref[0] ^ mask) * width, width)
        out_ref[:, pl.ds(start, width)] = ref[...].astype(jnp.float32)


def lay(place, parts, masks):
    rows, width = parts[0].shape
    vmem = pl.BlockSpec(memory_space=pltpu.VMEM)
    return pl.pallas_call(
        functools.partial(lay_kernel, masks),
        out_shape=jax.ShapeDtypeStruct((rows, width * len(parts)), jnp.float32),
        in_specs=[pl.BlockSpec(memory_space=pltpu.SMEM)] + [vmem] * len(parts),
        out_specs=vmem,
        name="lay",
    )(place, *parts)


def wide_form(design, row_signs, kept_rows):
    data = design[0]
    columns = data.shape[1]
    keep = kept_rows.shape[1]
    groups, members = lax.axis_size("grp"), lax.axis_size("inner")
    width = columns // members
    scale = 1.0 / (64.0 * math.sqrt(keep))
    place = jnp.stack([lax.axis_index("inner"), lax.axis_index("grp")]).astype(jnp.int32)
    make = functools.partial(contribution, place, kept_rows, row_signs, data, width)
    far = list(range(2, members, 2))
    order = far + [0]
    sums = {}
    for start in range(0, len(order), 2):
        pair = order[start : start + 2]
        sent = make([mask ^ 1 for mask in pair], jnp.bfloat16)
        arrived = swap(sent, "inner", 1)
        own = make(pair, jnp.float32)
        for index, mask in enumerate(pair):
            sums[mask] = own[index] + arrived[index].astype(jnp.float32)
    moved = [swap(sums[mask].astype(jnp.bfloat16), "inner", mask) for mask in far]

    panel = panel_contribution(place, kept_rows, row_signs, data)
    for axis, size in (("inner", members), ("grp", groups)):
        mask = 1
        while mask < size:
            panel = panel + swap(panel, axis, mask)
            mask *= 2
    vectors, weights = factor(panel, scale)

    *sends, own, product = spread(place, vectors, sums[0], moved, groups, scale)
    got = [swap(value, "grp", index + 1) for index, value in enumerate(sends)]
    done = apply(place, vectors, weights, own, product, got)
    parts = [done] + [swap(done, "inner", mask) for mask in far]
    masks = [0] + far
    parts += [swap(part, "inner", 1) for part in parts]
    masks += [mask ^ 1 for mask in masks]
    return lay(place, parts, masks)


def power_of_two(size):
    return size & (size - 1) == 0


def solution(mesh):
    groups, members = mesh.shape["grp"], mesh.shape["inner"]

    def on_device(design, row_signs, kept_rows):
        block_count, local_rows, columns = design.shape
        keep = kept_rows.shape[1]
        fits = (
            block_count == 1
            and power_of_two(groups)
            and power_of_two(members)
            and members >= 4
            and groups >= 2
            and columns % (members * LANES) == 0
            and local_rows % LOW == 0
            and local_rows // LOW < 8
            and keep % (groups * LANES) == 0
            and keep % 512 == 0
        )
        form = wide_form if fits else plain_form
        return form(design, row_signs, kept_rows)

    return jax.shard_map(
        on_device,
        mesh=mesh,
        in_specs=(P("inner", "grp", None), P("inner", "grp"), P("inner", None)),
        out_specs=P("grp", None),
        check_vma=False,
    )
```

```python
import functools
import math

import jax
import jax.numpy as jnp
from jax import lax
from jax.experimental import pallas as pl
from jax.experimental.pallas import tpu as pltpu
from jax.sharding import PartitionSpec as P

COLS_DONE = 8
LANES = 128
LOW = 256

epsilon = 1e-06


def sign_table(row_ids, col_ids):
    common_bits = jnp.bitwise_and(row_ids[:, None], col_ids[None, :])
    ones_total = jnp.zeros(common_bits.shape, jnp.int32)
    for bit_pos in range(4):
        ones_total = ones_total + jnp.bitwise_and(jnp.right_shift(common_bits, bit_pos), 1)
    return 1.0 - 2.0 * jnp.bitwise_and(ones_total, 1).astype(jnp.float32)


def pick_rows(table_rows, chosen_rows):
    return jnp.take(table_rows, chosen_rows, axis=0)


def plain_form(design, row_signs, kept_rows):
    block_count, local_rows, columns = design.shape
    keep_count = kept_rows.shape[1]
    groups = lax.axis_size("grp")
    owned_rows = keep_count // groups
    highest = lax.Precision.HIGHEST
    sixteen = jnp.arange(16, dtype=jnp.int32)
    hadamard = sign_table(sixteen, sixteen).astype(jnp.bfloat16)
    flipped = (design * (1 - 2 * row_signs).astype(jnp.float32)[:, :, None]).astype(jnp.bfloat16)
    lowest = flipped.reshape(block_count * local_rows // 16, 16, columns)
    first_pass = jnp.einsum(
        "hc,ncd->nhd", hadamard, lowest, preferred_element_type=jnp.float32
    ).astype(jnp.bfloat16)
    middle_view = first_pass.reshape(block_count * local_rows // 256, 16, 16, columns)
    second_pass = jnp.einsum(
        "hb,mbcd->mhcd", hadamard, middle_view, preferred_element_type=jnp.float32
    ).astype(jnp.bfloat16)
    second_pass = second_pass.reshape(block_count, local_rows, columns)
    gathered_rows = lax.all_to_all(second_pass, "grp", split_axis=2, concat_axis=1, tiled=True)
    col_count = gathered_rows.shape[2]
    by_piece = gathered_rows.reshape(block_count, 16, 256, col_count)
    mixed_rows = jnp.einsum("ha,nakd->nhkd", hadamard, by_piece, preferred_element_type=jnp.float32)
    mixed_rows = mixed_rows.reshape(block_count, 16 * 256, col_count)
    picked = jax.vmap(pick_rows)(mixed_rows, kept_rows)
    partial_value = jnp.sum(picked, axis=0)
    summed = lax.psum(partial_value, "inner")
    sketch = lax.all_to_all(summed, "grp", split_axis=0, concat_axis=1, tiled=True)
    sketch = sketch * (1.0 / (64.0 * math.sqrt(keep_count)))
    row_base = lax.axis_index("grp") * owned_rows
    global_rows = row_base + jnp.arange(owned_rows, dtype=jnp.int32)

    def reflect(col_index, current):
        column = jnp.where(global_rows >= col_index, current[:, col_index], 0.0)
        is_pivot = (global_rows == col_index).astype(jnp.float32)
        norm_sq, crossed, pivot_row = lax.psum(
            (
                jnp.sum(column * column),
                jnp.dot(column, current, precision=highest),
                jnp.dot(is_pivot, current, precision=highest),
            ),
            "grp",
        )
        pivot_value = pivot_row[col_index]
        head_value = -jnp.where(pivot_value >= 0, 1.0, -1.0) * jnp.sqrt(norm_sq)
        length = 2.0 * (norm_sq - head_value * pivot_value) + epsilon
        projected_row = crossed - head_value * pivot_row
        vector = column - head_value * is_pivot
        return current - vector[:, None] * (2.0 * projected_row / length)[None, :]

    return lax.fori_loop(0, COLS_DONE, reflect, sketch)


def swap(value, axis, mask):
    pairs = [(place, place ^ mask) for place in range(lax.axis_size(axis))]
    return lax.ppermute(value, axis, pairs)


def odd_ones(bits):
    bits = bits ^ (bits >> 2)
    bits = bits ^ (bits >> 1)
    return bits & 1


def low_hadamard(shift):
    row = lax.broadcasted_iota(jnp.int32, (LOW, LOW), 0)
    col = lax.broadcasted_iota(jnp.int32, (LOW, LOW), 1)
    signs = 1 - 2 * odd_ones((row & col) >> shift & 15)
    same = ((row ^ col) & (255 - (15 << shift))) == 0
    return jnp.where(same, signs, 0).astype(jnp.float32)


def resident(kernel, name, outs, args, scratch=(), spaces=None, out_spaces=None, mebibytes=16):
    here = pl.BlockSpec(memory_space=pltpu.VMEM)
    return pl.pallas_call(
        kernel,
        out_shape=outs,
        in_specs=spaces or [here] * len(args),
        out_specs=out_spaces or (here,) * len(outs),
        scratch_shapes=scratch,
        compiler_params=pltpu.CompilerParams(vmem_limit_bytes=mebibytes << 20),
        name=name,
    )(*args)


def front_kernel(kept_far, signs_far, data_ref, mixed_ref, table_ref, panel_ref, kept_ref, signs_ref, raw_ref, arrived):
    keep = kept_ref.shape[1]
    pieces = mixed_ref.shape[0] // LOW
    small = [
        pltpu.make_async_copy(kept_far, kept_ref, arrived.at[pieces]),
        pltpu.make_async_copy(signs_far, signs_ref, arrived.at[pieces + 1]),
    ]
    copies = []
    for piece in range(pieces):
        rows = pl.ds(piece * LOW, LOW)
        copies.append(pltpu.make_async_copy(data_ref.at[0, rows, :], raw_ref.at[rows, :], arrived.at[piece]))
    for copy in small + copies:
        copy.start()
    for copy in small:
        copy.wait()
    first_piece = lax.axis_index("grp") * pieces
    kept = jnp.broadcast_to(kept_ref[...], (8, keep))
    line = lax.broadcasted_iota(jnp.int32, kept.shape, 0)
    signs = 1 - 2 * odd_ones((kept >> 8) & (first_piece + line))
    packed = jnp.where(line < pieces, signs, kept & 255).astype(jnp.float32)
    step = 512
    for start in range(0, keep, step):
        tall = packed[:, start : start + step].T
        lane = lax.broadcasted_iota(jnp.int32, (step, LOW), 1).astype(jnp.float32)
        hit = tall[:, pieces : pieces + 1] == lane
        for piece in range(pieces):
            part = jnp.where(hit, tall[:, piece : piece + 1], 0.0).astype(jnp.bfloat16)
            table_ref[start : start + step, piece * LOW : (piece + 1) * LOW] = part
    inner_table = low_hadamard(0)
    outer_table = low_hadamard(4).astype(jnp.bfloat16)
    leads = []
    for piece in range(pieces):
        rows = slice(piece * LOW, (piece + 1) * LOW)
        flips = (1 - 2 * signs_ref[:, rows]).astype(jnp.float32)
        table = (inner_table * flips).astype(jnp.bfloat16)
        copies[piece].wait()
        first = jnp.dot(table, raw_ref[rows, :].astype(jnp.bfloat16), preferred_element_type=jnp.float32)
        second = jnp.dot(outer_table, first.astype(jnp.bfloat16), preferred_element_type=jnp.float32)
        second = second.astype(jnp.bfloat16)
        mixed_ref[rows, :] = second
        leads.append(second[:, :LANES].astype(jnp.float32).T[:16].astype(jnp.bfloat16))
    lead = jnp.concatenate(leads, axis=1)
    for start in range(0, keep, step):
        rows = slice(start, start + step)
        part = lax.dot_general(
            lead, table_ref[rows, :], (((1,), (1,)), ((), ())), preferred_element_type=jnp.float32
        )
        panel_ref[:, rows] = part[:COLS_DONE]


def front(kept, signs, design):
    _, rows, columns = design.shape
    keep = kept.shape[1]
    outs = (
        pltpu.VMEM((rows, columns), jnp.bfloat16),
        pltpu.VMEM((keep, rows), jnp.bfloat16),
        pltpu.VMEM((COLS_DONE, keep), jnp.float32),
    )
    scratch = [
        pltpu.VMEM(kept.shape, jnp.int32),
        pltpu.VMEM(signs.shape, jnp.int32),
        pltpu.VMEM((rows, columns), jnp.float32),
        pltpu.SemaphoreType.DMA((rows // LOW + 2,)),
    ]
    spaces = [pl.BlockSpec(memory_space=pltpu.HBM)] * 3
    return resident(front_kernel, "front", outs, (kept, signs, design), scratch, spaces, mebibytes=56)


def addend_kernel(masks, width, has_arrived, has_panel, table_ref, mixed_ref, *refs):
    refs = list(refs)
    arrived = [refs.pop(0) for _ in masks] if has_arrived else []
    panels = [refs.pop(0) for _ in range(2)] if has_panel else []
    member = lax.axis_index("inner")
    if has_panel:
        refs.pop()[...] = panels[0][...] + panels[1][...]
    parts = []
    for mask in masks:
        parts.append(mixed_ref[:, pl.ds(pl.multiple_of((member ^ mask) * width, width), width)])
    part = jnp.dot(table_ref[...], jnp.concatenate(parts, axis=1), preferred_element_type=jnp.float32)
    for index, out_ref in enumerate(refs):
        value = part[:, index * width : (index + 1) * width]
        if arrived:
            value = value + arrived[index][...].astype(jnp.float32)
        out_ref[...] = value.astype(out_ref.dtype)


def addend(table, mixed, masks, width, dtypes, arrived=(), panels=()):
    keep = table.shape[0]
    outs = tuple(pltpu.VMEM((keep, width), dtype) for dtype in dtypes)
    outs += tuple(pltpu.VMEM(panel.shape, panel.dtype) for panel in panels[:1])
    kernel = functools.partial(addend_kernel, masks, width, bool(arrived), bool(panels))
    return resident(kernel, "addend", outs, (table, mixed, *arrived, *panels))


def factor_kernel(scale, panel_ref, other_ref, vectors_ref, weights_ref):
    current = (panel_ref[...] + other_ref[...]) * scale
    count, keep = current.shape
    lane = lax.broadcasted_iota(jnp.int32, (1, keep), 1)
    line = lax.broadcasted_iota(jnp.int32, (count, 1), 0)
    short = lax.broadcasted_iota(jnp.int32, (1, LANES), 1)
    vectors = jnp.zeros((count, keep), jnp.float32)
    weights = jnp.zeros((count, LANES), jnp.float32)
    for j in range(count):
        column = jnp.where(lane >= j, current[j : j + 1, :], 0.0)
        is_pivot = lane == j
        crossed = jnp.sum(current * column, axis=1, keepdims=True)
        pivot_row = jnp.sum(jnp.where(is_pivot, current, 0.0), axis=1, keepdims=True)
        norm_sq = crossed[j : j + 1, :]
        pivot = pivot_row[j : j + 1, :]
        head = jnp.where(pivot >= 0, -1.0, 1.0) * jnp.sqrt(norm_sq)
        length = 2.0 * (norm_sq - head * pivot) + epsilon
        vector = column - jnp.where(is_pivot, head, 0.0)
        projected = crossed - head * pivot_row
        current = current - (2.0 * projected / length) * vector
        shared = jnp.sum(vectors * vector, axis=1, keepdims=True)
        unit = jnp.where(short == j, 1.0, 0.0)
        row = (2.0 / length) * (unit - jnp.sum(shared * weights, axis=0, keepdims=True))
        vectors = jnp.where(line == j, vector, vectors)
        weights = jnp.where(line == j, row, weights)
    vectors_ref[...] = vectors
    weights_ref[...] = weights


def factor(panel, other, scale):
    count, keep = panel.shape
    outs = (pltpu.VMEM((count, keep), jnp.float32), pltpu.VMEM((count, LANES), jnp.float32))
    return resident(functools.partial(factor_kernel, scale), "factor", outs, (panel, other))


def split_two(value):
    high = value.astype(jnp.bfloat16)
    low = (value - high.astype(jnp.float32)).astype(jnp.bfloat16)
    return jnp.concatenate([high, low], axis=0)


def spread_kernel(scale, arrived_count, vectors_ref, base_ref, *refs):
    arrived, outs = refs[:arrived_count], refs[arrived_count:]
    *send_refs, own_ref, product_ref = outs
    rows = own_ref.shape[0]
    count = vectors_ref.shape[0]
    group = lax.axis_index("grp")

    def total(window):
        value = base_ref[window, :]
        for ref in arrived:
            value = value + ref[window, :].astype(jnp.float32)
        return value * scale

    both = jnp.zeros((2 * count, own_ref.shape[1]), jnp.float32)
    for index in range(len(send_refs) + 1):
        start = pl.multiple_of((group ^ index) * rows, rows)
        value = total(pl.ds(start, rows))
        short = value.astype(jnp.bfloat16)
        if index:
            send_refs[index - 1][:rows, :] = short
        else:
            own_ref[...] = value
        pair = split_two(vectors_ref[:, pl.ds(start, rows)])
        both = both + jnp.dot(pair, short, preferred_element_type=jnp.float32)
    product = both[:count] + both[count:]
    product_ref[...] = product
    pair = split_two(product)
    for send_ref in send_refs:
        send_ref[rows:, :] = pair


def spread(vectors, base, arrived, groups, scale):
    keep, width = base.shape
    count = vectors.shape[0]
    rows = keep // groups
    outs = [pltpu.VMEM((rows + 2 * count, width), jnp.bfloat16)] * (groups - 1)
    outs += [pltpu.VMEM((rows, width), jnp.float32), pltpu.VMEM((count, width), jnp.float32)]
    kernel = functools.partial(spread_kernel, scale, len(arrived))
    return resident(kernel, "spread", tuple(outs), (vectors, base, *arrived))


def apply_kernel(vectors_ref, weights_ref, own_ref, product_ref, *refs):
    *arrived, out_ref = refs
    rows = own_ref.shape[0]
    count = vectors_ref.shape[0]
    value = own_ref[...]
    product = product_ref[...]
    for ref in arrived:
        value = value + ref[:rows, :].astype(jnp.float32)
        pair = ref[rows:, :].astype(jnp.float32)
        product = product + (pair[:count] + pair[count:])
    highest = lax.Precision.HIGHEST
    multipliers = jnp.dot(
        weights_ref[:, :count], product, precision=highest, preferred_element_type=jnp.float32
    )
    window = pl.ds(pl.multiple_of(lax.axis_index("grp") * rows, rows), rows)
    vectors = vectors_ref[:, window]
    update = lax.dot_general(
        vectors, multipliers, (((0,), (0,)), ((), ())), precision=highest, preferred_element_type=jnp.float32
    )
    out_ref[...] = (value - update).astype(jnp.bfloat16)


def apply(vectors, weights, own, product, arrived):
    outs = (pltpu.VMEM(own.shape, jnp.bfloat16),)
    return resident(apply_kernel, "apply", outs, (vectors, weights, own, product, *arrived))[0]


def lay_kernel(masks, *refs):
    parts, (out_ref, wide_ref, left) = refs[: len(masks)], refs[len(masks) :]
    width = parts[0].shape[1]
    copies = []
    for index, mask in enumerate(masks):
        start = pl.multiple_of((lax.axis_index("inner") ^ mask) * width, width)
        wide_ref[index] = parts[index][...].astype(jnp.float32)
        copies.append(
            pltpu.make_async_copy(wide_ref.at[index], out_ref.at[:, pl.ds(start, width)], left.at[index])
        )
        copies[-1].start()
    for copy in copies:
        copy.wait()


def lay(parts, masks):
    rows, width = parts[0].shape
    outs = (jax.ShapeDtypeStruct((rows, width * len(parts)), jnp.float32),)
    scratch = [pltpu.VMEM((len(parts), rows, width), jnp.float32), pltpu.SemaphoreType.DMA((len(parts),))]
    away = (pl.BlockSpec(memory_space=pl.ANY),)
    return resident(functools.partial(lay_kernel, masks), "lay", outs, parts, scratch, None, away)[0]


def wide_form(design, row_signs, kept_rows):
    columns = design.shape[2]
    keep = kept_rows.shape[1]
    groups, members = lax.axis_size("grp"), lax.axis_size("inner")
    width = columns // members
    scale = 1.0 / (64.0 * math.sqrt(keep))
    short, full = jnp.bfloat16, jnp.float32
    mixed, table, panel = front(kept_rows, row_signs, design)

    steps = [("inner", 1 << bit) for bit in range(members.bit_length() - 1)]
    steps += [("grp", 1 << bit) for bit in range(groups.bit_length() - 1)]
    far = list(range(2, members, 2))
    order = far + [0]
    pairs = [order[start : start + 2] for start in range(0, len(order), 2)]
    work = [([mask ^ 1 for mask in pair], [short] * 2, None) for pair in pairs]
    work += [(pair, [short if mask else full for mask in pair], index) for index, pair in enumerate(pairs)]
    arrived, sums = [], {}
    waiting = swap(panel, *steps.pop(0))
    for turn, (masks, dtypes, index) in enumerate(work):
        panels = (panel, waiting) if turn and len(steps) > 1 else ()
        got = arrived[index] if index is not None else ()
        values = list(addend(table, mixed, masks, width, dtypes, got, panels))
        if panels:
            panel = values.pop()
            waiting = swap(panel, *steps.pop(0))
        if index is None:
            arrived.append([swap(value, "inner", 1) for value in values])
        else:
            sums.update(zip(masks, values))
    moved = [swap(sums[mask], "inner", mask) for mask in far]
    while steps:
        panel = panel + waiting
        waiting = swap(panel, *steps.pop(0))
    vectors, weights = factor(panel, waiting, scale)

    *sends, own, product = spread(vectors, sums[0], moved, groups, scale)
    got = [swap(value, "grp", index + 1) for index, value in enumerate(sends)]
    done = apply(vectors, weights, own, product, got)
    parts = [done] + [swap(done, "inner", mask) for mask in far]
    masks = [0] + far
    parts += [swap(part, "inner", 1) for part in parts]
    masks += [mask ^ 1 for mask in masks]
    return lay(parts, masks)


def power_of_two(size):
    return size & (size - 1) == 0


def solution(mesh):
    groups, members = mesh.shape["grp"], mesh.shape["inner"]

    def on_device(design, row_signs, kept_rows):
        block_count, local_rows, columns = design.shape
        keep = kept_rows.shape[1]
        fits = (
            block_count == 1
            and power_of_two(groups)
            and power_of_two(members)
            and members >= 4
            and groups >= 2
            and columns % (members * LANES) == 0
            and local_rows % LOW == 0
            and local_rows // LOW < 8
            and keep % (groups * LANES) == 0
            and keep % 512 == 0
        )
        form = wide_form if fits else plain_form
        return form(design, row_signs, kept_rows)

    return jax.shard_map(
        on_device,
        mesh=mesh,
        in_specs=(P("inner", "grp", None), P("inner", "grp"), P("inner", None)),
        out_specs=P("grp", None),
        check_vma=False,
    )
```
